256 devices in a mesh: dp: 16 (over z, y_hi), ctx: 16 (over x, y_lo, core).
Axes of the slice: x: 4, y: 4 (y_hi: 2, y_lo: 2; y = y_hi * 2 + y_lo), z: 8, core: 2. Of those that a mesh axis runs over, the one named last changes fastest.
Arguments:
- queries: bfloat16 [32768, 2048], P(('dp', 'ctx')), parts along dimension 0, may hold values from -16 to 16
- keys: bfloat16 [32768, 512], P(('dp', 'ctx')), parts along dimension 0, may hold values from -16 to 16
- values: bfloat16 [32768, 512], P(('dp', 'ctx')), parts along dimension 0, may hold values from -6 to 6
- out_grad: bfloat16 [32768, 2048], P(('dp', 'ctx')), parts along dimension 0, may hold values from -6 to 6
- span_of: int32 [512], P('dp'), parts along dimension 0, may hold values from 0 to 31, each once
Outputs:
- query_grad: bfloat16 [32768, 2048], P(('dp', 'ctx')), parts along dimension 0
- key_grad: bfloat16 [32768, 512], P(('dp', 'ctx')), parts along dimension 0
- value_grad: bfloat16 [32768, 512], P(('dp', 'ctx')), parts along dimension 0
The draws below stay inside these ranges and needn't reach their ends.
There are 16 independent parts, one for each index of `dp`. The reference program is written for one: setup_inputs(seed, part) draws one part's arguments, and reference() takes and returns one part's arrays. A program takes and returns all parts, laid end to end along the dimension named above; each array names one. Nothing has to cross between parts.
Inputs may be any that keep to these rules, and one draw needn't show every extreme that they name: `span_of`: each of the 32 spans of the document stands in exactly one half of one device's rows.
All inputs are finite; a program needn't handle non-finite values.
Results may differ from the reference program's by a relative error of at most 0.0069.
Values may be sent and summed in bfloat16 or wider, within the bound.
No kernel may reach another device: no remote copies, remote signals or barrier semaphores. Data moves between devices by JAX's collectives and lax.ppermute only.
A program may use at most 64 MiB of HBM per device.

```python
import math
import jax
import jax.numpy as jnp
from jax import lax

HEADS = 16
KV_HEADS = 4
HEAD = 128
TOK_DEV = 128
SEQ = 2048
N_CTX = 16


def draw_queries(key, part):
    result = jnp.clip(jax.random.normal(jax.random.fold_in(key, 1), (SEQ, HEADS * HEAD), jnp.float32), -4.0, 4.0)
    return result.astype(jnp.bfloat16)


def draw_keys(key, part):
    result = jnp.clip(jax.random.normal(jax.random.fold_in(key, 3), (SEQ, KV_HEADS * HEAD), jnp.float32), -4.0, 4.0)
    return result.astype(jnp.bfloat16)


def block_levels(key, extent, pieces, low, largest):
    def one(axis_at, blocks):
        steps = jax.random.uniform(jax.random.fold_in(jax.random.fold_in(key, 6), axis_at), (blocks,), jnp.float32, low / len(pieces), largest / len(pieces))
        return jnp.repeat(jnp.exp(steps), extent[axis_at] // blocks).reshape((-1,) + (1,) * (len(extent) - axis_at - 1))

    level = one(*pieces[0])
    for cut in pieces[1:]:
        level = level * one(*cut)
    return level


def normal_values(stream_key, extent, scale, bound, cuts=(), held_as=jnp.bfloat16):
    values = jax.random.normal(stream_key, extent, jnp.float32) * scale
    if len(cuts) > 0:
        values = block_levels(stream_key, extent, cuts, -0.22, 0.18) * values
    return jnp.clip(values, min=-bound, max=bound).astype(held_as)


def setup_inputs(seed: int = 0, part: int = 0) -> dict:
    streams_of = jax.random.split(jax.random.key(seed), 6)
    part_splits = jax.random.split(jax.random.fold_in(streams_of[5], part), 6)
    return {
        "queries": draw_queries(jax.random.fold_in(jax.random.fold_in(streams_of[5], part), 71), part),
        "keys": draw_keys(jax.random.fold_in(jax.random.fold_in(streams_of[5], part), 71), part),
        "values": normal_values(part_splits[2], (SEQ, KV_HEADS * HEAD), 1.0, 6.0, ((0, 16),)),
        "out_grad": normal_values(part_splits[3], (SEQ, HEADS * HEAD), 1.0, 6.0, ((0, 16),)),
        "span_of": jax.random.permutation(part_splits[4], 2 * N_CTX).astype(jnp.int32),
    }


def reference(queries, keys, values, out_grad, span_of):
    half_rows = TOK_DEV // 2
    repeat = HEADS // KV_HEADS
    scaling = 1.0 / math.sqrt(HEAD)
    row_ids = jnp.arange(SEQ, dtype=jnp.int32)
    positions = span_of[row_ids // half_rows] * half_rows + row_ids % half_rows
    visible = positions[None, :] <= positions[:, None]
    query_groups = queries.reshape(SEQ, KV_HEADS, repeat, HEAD).transpose(1, 2, 0, 3)
    grad_groups = out_grad.reshape(SEQ, KV_HEADS, repeat, HEAD).transpose(1, 2, 0, 3)
    key_groups = keys.reshape(SEQ, KV_HEADS, HEAD).transpose(1, 0, 2)
    value_groups = values.reshape(SEQ, KV_HEADS, HEAD).transpose(1, 0, 2)

    def one_group(operands):
        query_part, grad_part, key_part, value_part = operands
        query_full = query_part.astype(jnp.float32)
        grad_full = grad_part.astype(jnp.float32)
        key_full = key_part.astype(jnp.float32)
        value_full = value_part.astype(jnp.float32)
        scores = jnp.einsum('rqd,kd->rqk', query_full, key_full) * scaling
        scores = jnp.where(visible, scores, -jnp.inf)
        row_lse = jax.nn.logsumexp(scores, axis=-1)
        weights = jnp.where(visible, jnp.exp(scores - row_lse[..., None]), 0.0)
        weight_half = lax.optimization_barrier(weights.astype(jnp.bfloat16)).astype(jnp.float32)
        attended = jnp.einsum('rqk,kd->rqd', weight_half, value_full)
        delta = lax.optimization_barrier(jnp.sum(grad_full * attended, axis=-1))
        pushes = jnp.einsum('rqd,kd->rqk', grad_full, value_full)
        slopes = (weights * (pushes - delta[..., None]) * scaling).astype(jnp.bfloat16)
        slopes = lax.optimization_barrier(slopes).astype(jnp.float32)
        query_grad = jnp.einsum('rqk,kd->rqd', slopes, key_full).astype(jnp.bfloat16)
        key_grad = jnp.einsum('rqk,rqd->kd', slopes, query_full).astype(jnp.bfloat16)
        value_grad = jnp.einsum('rqk,rqd->kd', weight_half, grad_full).astype(jnp.bfloat16)
        return (query_grad, key_grad, value_grad)
    query_parts, key_parts, value_parts = lax.map(one_group, (query_groups, grad_groups, key_groups, value_groups))
    query_grad = query_parts.transpose(2, 0, 1, 3).reshape(SEQ, HEADS * HEAD)
    key_grad = key_parts.transpose(1, 0, 2).reshape(SEQ, KV_HEADS * HEAD)
    value_grad = value_parts.transpose(1, 0, 2).reshape(SEQ, KV_HEADS * HEAD)
    return (query_grad, key_grad, value_grad)
```

```python
import math

import jax
import jax.numpy as jnp
from jax import lax
from jax.experimental import pallas as pl
from jax.experimental.pallas import tpu as pltpu
from jax.sharding import Mesh, PartitionSpec as P

HEAD = 128
GROUPS = 4
REPEAT = 4
TOK = 128
HALF = 64
SEQ = 2048
TILE = 512
ROWS = REPEAT * HALF
WIDE = REPEAT * HEAD
NEG_FILL = -1e30
F32 = jnp.float32
BF16 = jnp.bfloat16
VMEM = pl.BlockSpec(memory_space=pltpu.VMEM)
SMEM = pl.BlockSpec(memory_space=pltpu.SMEM)
PARAMS = pltpu.CompilerParams(vmem_limit_bytes=48 * 1024 * 1024)


def struct(shape, dtype):
    return jax.ShapeDtypeStruct(shape, dtype)


def cut_kv_kernel(place, keys, values, *pieces):
    for step in range(GROUPS):
        column = pl.multiple_of(((place[0] + step) % GROUPS) * HEAD, HEAD)
        pieces[step][:, :HEAD] = keys[:, pl.ds(column, HEAD)]
        pieces[step][:, HEAD:] = values[:, pl.ds(column, HEAD)]


def cut_kv(place, keys, values):
    return pl.pallas_call(
        cut_kv_kernel,
        out_shape=[struct((TOK, 2 * HEAD), BF16)] * GROUPS,
        in_specs=[SMEM, VMEM, VMEM],
        out_specs=[VMEM] * GROUPS,
        name="cut_kv",
    )(place, keys, values)


def cut_rows_kernel(place, queries, out_grad, *pieces):
    for step in range(GROUPS):
        column = pl.multiple_of(((place[0] + step) % GROUPS) * WIDE, WIDE)
        pieces[step][:, :WIDE] = queries[:, pl.ds(column, WIDE)]
        pieces[step][:, WIDE:] = out_grad[:, pl.ds(column, WIDE)]


def cut_rows(place, queries, out_grad):
    return pl.pallas_call(
        cut_rows_kernel,
        out_shape=[struct((TOK, 2 * WIDE), BF16)] * GROUPS,
        in_specs=[SMEM, VMEM, VMEM],
        out_specs=[VMEM] * GROUPS,
        name="cut_rows",
    )(place, queries, out_grad)


def nt(a, b):
    return lax.dot_general(a, b, (((1,), (1,)), ((), ())), preferred_element_type=F32)


def nn(a, b):
    return lax.dot_general(a, b, (((1,), (0,)), ((), ())), preferred_element_type=F32)


def fold(tile, op):
    return op(tile.reshape(TILE // 8, 8, ROWS), axis=0)


def attention_kernel(
    place, spans, r0, r1, r2, r3, kv00, kv10, kv01, kv11,
    dq0, dq1, dq2, dq3, keep, send,
    ks, vs, kt, rows, dqs, es, ps, dk, dv,
):
    x, y, c = place[0], place[1], place[2]
    scaling = HEAD ** (-0.5)
    to_base2 = scaling * math.log2(math.e)

    def start_of(step, dy, dc, half):
        owner = ((x - step) % GROUPS) * 4 + (y ^ dy) * 2 + (c ^ dc)
        return spans[2 * owner + half]

    kv_sets = (((0, 0), kv00), ((1, 0), kv10), ((0, 1), kv01), ((1, 1), kv11))
    for (dy, dc), ref in kv_sets:
        for step in range(GROUPS):
            for half in range(2):
                base = pl.multiple_of(start_of(step, dy, dc, half) * HALF, HALF)
                block = ref[step, half * HALF : (half + 1) * HALF]
                ks[pl.ds(base, HALF), :] = block[:, :HEAD]
                vs[pl.ds(base, HALF), :] = block[:, HEAD:]
    for tile in range(SEQ // TILE):
        kt[:, tile * TILE : (tile + 1) * TILE] = ks[tile * TILE : (tile + 1) * TILE].T
    for step, ref in enumerate((r0, r1, r2, r3)):
        for half in range(2):
            rows[2 * step + half] = ref[half * HALF : (half + 1) * HALF]
    dk[...] = jnp.zeros_like(dk)
    dv[...] = jnp.zeros_like(dv)
    key_iota = lax.broadcasted_iota(jnp.int32, (TILE, ROWS), 0)
    lane_token = lax.broadcasted_iota(jnp.int32, (TILE, ROWS), 1) % HALF
    lead = key_iota - lane_token

    def one_span(turn, unused):
        span = start_of(turn // 2, 0, 0, turn % 2)
        tiles = span * HALF // TILE + 1
        block = rows[turn]
        q = jnp.concatenate([block[:, h * HEAD : (h + 1) * HEAD] for h in range(REPEAT)], axis=0)
        g = jnp.concatenate(
            [block[:, WIDE + h * HEAD : WIDE + (h + 1) * HEAD] for h in range(REPEAT)], axis=0
        )

        def at(tile):
            return pl.ds(pl.multiple_of(tile * TILE, TILE), TILE)

        def score(tile, peak):
            s = nt(ks[at(tile), :], q)
            s = jnp.where(lead <= span * HALF - tile * TILE, s, NEG_FILL)
            es[at(tile), :] = s
            ps[at(tile), :] = nt(vs[at(tile), :], g)
            return jnp.maximum(peak, fold(s, jnp.max))

        peak = lax.fori_loop(0, tiles, score, jnp.full((8, ROWS), NEG_FILL, F32))
        peak = jnp.max(peak, axis=0, keepdims=True)

        def exponent(tile, total):
            e = jnp.exp2((es[at(tile), :] - peak) * to_base2)
            es[at(tile), :] = e
            return total + fold(e, jnp.sum)

        total = lax.fori_loop(0, tiles, exponent, jnp.zeros((8, ROWS), F32))
        inverse = 1.0 / jnp.sum(total, axis=0, keepdims=True)

        def value_side(tile, delta):
            w = (es[at(tile), :] * inverse).astype(BF16)
            dv[at(tile), :] += nn(w, g)
            return delta + fold(w.astype(F32) * ps[at(tile), :], jnp.sum)

        delta = lax.fori_loop(0, tiles, value_side, jnp.zeros((8, ROWS), F32))
        delta = jnp.sum(delta, axis=0, keepdims=True)
        factor = inverse * scaling

        def key_side(tile, dq_t):
            slopes = (es[at(tile), :] * factor * (ps[at(tile), :] - delta)).astype(BF16)
            dk[at(tile), :] += nn(slopes, q)
            return dq_t + nn(kt[:, at(tile)], slopes)

        dq_t = lax.fori_loop(0, tiles, key_side, jnp.zeros((HEAD, ROWS), F32))
        dq = dq_t.T.astype(BF16)
        for h in range(REPEAT):
            dqs[turn, :, h * HEAD : (h + 1) * HEAD] = dq[h * HALF : (h + 1) * HALF]
        return unused

    lax.fori_loop(0, 2 * GROUPS, one_span, 0)
    for step, ref in enumerate((dq0, dq1, dq2, dq3)):
        for half in range(2):
            ref[half * HALF : (half + 1) * HALF] = dqs[2 * step + half]
    for dc, ref in ((0, keep), (1, send)):
        for dy in range(2):
            for step in range(GROUPS):
                for half in range(2):
                    base = pl.multiple_of(start_of(step, dy, dc, half) * HALF, HALF)
                    here = slice(half * HALF, (half + 1) * HALF)
                    ref[dy, step, here, :HEAD] = dk[pl.ds(base, HALF), :].astype(ref.dtype)
                    ref[dy, step, here, HEAD:] = dv[pl.ds(base, HALF), :].astype(ref.dtype)


def attention(place, spans, row_pieces, kv_sets):
    return pl.pallas_call(
        attention_kernel,
        out_shape=[struct((TOK, WIDE), BF16)] * GROUPS
        + [
            struct((2, GROUPS, TOK, 2 * HEAD), F32),
            struct((2, GROUPS, TOK, 2 * HEAD), BF16),
        ],
        in_specs=[SMEM, SMEM] + [VMEM] * 8,
        out_specs=[VMEM] * 6,
        scratch_shapes=[
            pltpu.VMEM((SEQ, HEAD), BF16),
            pltpu.VMEM((SEQ, HEAD), BF16),
            pltpu.VMEM((HEAD, SEQ), BF16),
            pltpu.VMEM((2 * GROUPS, HALF, 2 * WIDE), BF16),
            pltpu.VMEM((2 * GROUPS, HALF, WIDE), BF16),
            pltpu.VMEM((SEQ, ROWS), F32),
            pltpu.VMEM((SEQ, ROWS), F32),
            pltpu.VMEM((SEQ, HEAD), F32),
            pltpu.VMEM((SEQ, HEAD), F32),
        ],
        compiler_params=PARAMS,
        name="attention_backward",
    )(place, spans, *row_pieces, *kv_sets)


def join_rows_kernel(place, p0, p1, p2, p3, out):
    for step, ref in enumerate((p0, p1, p2, p3)):
        column = pl.multiple_of(((place[0] + step) % GROUPS) * WIDE, WIDE)
        out[:, pl.ds(column, WIDE)] = ref[...]


def join_rows(place, pieces):
    return pl.pallas_call(
        join_rows_kernel,
        out_shape=struct((TOK, GROUPS * WIDE), BF16),
        in_specs=[SMEM] + [VMEM] * GROUPS,
        out_specs=VMEM,
        name="join_rows",
    )(place, *pieces)


def join_kv_kernel(place, p0, p1, p2, p3, key_out, value_out):
    for step, ref in enumerate((p0, p1, p2, p3)):
        column = pl.multiple_of(((place[0] + step) % GROUPS) * HEAD, HEAD)
        key_out[:, pl.ds(column, HEAD)] = ref[:, :HEAD]
        value_out[:, pl.ds(column, HEAD)] = ref[:, HEAD:]


def join_kv(place, pieces):
    return pl.pallas_call(
        join_kv_kernel,
        out_shape=[struct((TOK, GROUPS * HEAD), BF16)] * 2,
        in_specs=[SMEM] + [VMEM] * GROUPS,
        out_specs=[VMEM] * 2,
        name="join_kv",
    )(place, *pieces)


def ahead(block, step):
    return lax.ppermute(block, "x", [(i, (i + step) % GROUPS) for i in range(GROUPS)])


def swap(block, axis):
    return lax.ppermute(block, axis, [(0, 1), (1, 0)])


def on_device(queries, keys, values, out_grad, spans):
    place = jnp.stack([lax.axis_index("x"), lax.axis_index("y"), lax.axis_index("c")])
    place = place.astype(jnp.int32)
    kv_cut = cut_kv(place, keys, values)
    kv_mine = jnp.stack([kv_cut[0]] + [ahead(kv_cut[step], step) for step in range(1, GROUPS)])
    row_cut = cut_rows(place, queries, out_grad)
    row_got = {0: row_cut[0]}
    for step in (1, 3, 2):
        row_got[step] = ahead(row_cut[step], step)
    kv_y = swap(kv_mine, "y")
    kv_c = swap(kv_mine, "c")
    kv_yc = swap(kv_y, "c")
    row_pieces = [row_got[step] for step in range(GROUPS)]
    dq0, dq1, dq2, dq3, keep, send = attention(
        place, spans, row_pieces, [kv_mine, kv_y, kv_c, kv_yc]
    )
    dq_pieces = (dq0, dq1, dq2, dq3)
    total = keep + swap(send, "c").astype(F32)
    from_y = swap(total[1].astype(BF16), "y")
    dq_home = {0: dq0}
    for step in (1, 3, 2):
        dq_home[step] = ahead(dq_pieces[step], GROUPS - step)
    query_grad = join_rows(place, [dq_home[step] for step in range(GROUPS)])
    summed = (total[0] + from_y.astype(F32)).astype(BF16)
    home = [summed[0]] + [ahead(summed[step], GROUPS - step) for step in range(1, GROUPS)]
    key_grad, value_grad = join_kv(place, home)
    return query_grad, key_grad, value_grad


def solution(mesh):
    split = Mesh(mesh.devices.reshape(-1, 4, 2, 2), ("dp", "x", "y", "c"))
    whole = P(("dp", "x", "y", "c"), None)
    return jax.shard_map(
        on_device,
        mesh=split,
        in_specs=(whole, whole, whole, whole, P("dp")),
        out_specs=(whole, whole, whole),
        check_vma=False,
    )
```

```python
import math
from functools import partial

import jax
import jax.numpy as jnp
from jax import lax
from jax.experimental import pallas as pl
from jax.experimental.pallas import tpu as pltpu
from jax.sharding import Mesh, PartitionSpec as P

HEAD = 128
GROUPS = 4
REPEAT = 4
TOK = 128
HALF = 64
SEQ = 2048
TILE = 256
PACK = 2
ROWS = PACK * REPEAT * HALF
WIDE = REPEAT * HEAD
NEG_FILL = -1e30
F32 = jnp.float32
BF16 = jnp.bfloat16
VMEM = pl.BlockSpec(memory_space=pltpu.VMEM)
ANY = pl.BlockSpec(memory_space=pl.ANY)
SMEM = pl.BlockSpec(memory_space=pltpu.SMEM)
PARAMS = pltpu.CompilerParams(vmem_limit_bytes=48 * 1024 * 1024)


LONG = pl.CostEstimate(flops=30_000_000_000, transcendentals=0, bytes_accessed=60_000_000)


def struct(shape, dtype):
    return jax.ShapeDtypeStruct(shape, dtype)


def cut_kv_kernel(keys, values, *pieces):
    x = lax.axis_index("x")
    for step in range(GROUPS):
        column = pl.multiple_of(((x + step) % GROUPS) * HEAD, HEAD)
        pieces[step][:, :HEAD] = keys[:, pl.ds(column, HEAD)]
        pieces[step][:, HEAD:] = values[:, pl.ds(column, HEAD)]


def cut_kv(keys, values):
    return pl.pallas_call(
        cut_kv_kernel,
        out_shape=[struct((TOK, 2 * HEAD), BF16)] * GROUPS,
        in_specs=[VMEM, VMEM],
        out_specs=[VMEM] * GROUPS,
        compiler_params=PARAMS,
        name="cut_kv",
    )(keys, values)


def cut_rows_kernel(queries, out_grad, *pieces):
    x = lax.axis_index("x")
    for step in range(1, GROUPS):
        column = pl.multiple_of(((x + step) % GROUPS) * WIDE, WIDE)
        pieces[step - 1][:, :WIDE] = queries[:, pl.ds(column, WIDE)]
        pieces[step - 1][:, WIDE:] = out_grad[:, pl.ds(column, WIDE)]


def cut_rows(queries, out_grad):
    return pl.pallas_call(
        cut_rows_kernel,
        out_shape=[struct((TOK, 2 * WIDE), BF16)] * (GROUPS - 1),
        in_specs=[VMEM, VMEM],
        out_specs=[VMEM] * (GROUPS - 1),
        compiler_params=PARAMS,
        name="cut_rows",
    )(queries, out_grad)


def arrived_kernel(r1, r2, r3, out):
    out[...] = r1[:8, :HEAD] + r2[:8, :HEAD] + r3[:8, :HEAD]


def arrived(pieces):
    return pl.pallas_call(
        arrived_kernel,
        out_shape=struct((8, HEAD), BF16),
        in_specs=[VMEM] * 3,
        out_specs=VMEM,
        cost_estimate=LONG,
        compiler_params=PARAMS,
        name="rows_arrived",
    )(*pieces)


def nt(a, b):
    return lax.dot_general(a, b, (((1,), (1,)), ((), ())), preferred_element_type=F32)


def nn(a, b):
    return lax.dot_general(a, b, (((1,), (0,)), ((), ())), preferred_element_type=F32)


def fold(tile, op):
    return op(tile.reshape(TILE // 8, 8, ROWS), axis=0)


def attention_kernel(
    spans, token, queries, out_grad, r1, r2, r3, kv00, kv10, kv01, kv11,
    dq0, dq1, dq2, dq3, keep, send,
    ks, vs, kt, rows, dqs, es, ps, dk, dv, order, mine, sems,
):
    x, y, c = lax.axis_index("x"), lax.axis_index("y"), lax.axis_index("c")
    here = pl.ds(pl.multiple_of(x * WIDE, WIDE), WIDE)
    fetches = [
        pltpu.make_async_copy(queries.at[:, here], mine.at[:, :WIDE], sems.at[0]),
        pltpu.make_async_copy(out_grad.at[:, here], mine.at[:, WIDE:], sems.at[1]),
    ]
    for fetch in fetches:
        fetch.start()
    scaling = HEAD ** (-0.5)
    to_base2 = scaling * math.log2(math.e)

    def start_of(step, dy, dc, half):
        owner = ((x - step) % GROUPS) * 4 + (y ^ dy) * 2 + (c ^ dc)
        return spans[2 * owner + half]

    kv_sets = (((0, 0), kv00), ((1, 0), kv10), ((0, 1), kv01), ((1, 1), kv11))
    for (dy, dc), ref in kv_sets:
        for step in range(GROUPS):
            for half in range(2):
                base = pl.multiple_of(start_of(step, dy, dc, half) * HALF, HALF)
                block = ref[step, half * HALF : (half + 1) * HALF]
                ks[pl.ds(base, HALF), :] = block[:, :HEAD]
                vs[pl.ds(base, HALF), :] = block[:, HEAD:]
    for tile in range(SEQ // TILE):
        kt[:, tile * TILE : (tile + 1) * TILE] = ks[tile * TILE : (tile + 1) * TILE].T
    for fetch in fetches:
        fetch.wait()
    for step, ref in enumerate((mine, r1, r2, r3)):
        for half in range(2):
            rows[2 * step + half] = ref[half * HALF : (half + 1) * HALF]
    turns = range(2 * GROUPS)
    own = [start_of(turn // 2, 0, 0, turn % 2) for turn in turns]
    for turn in turns:
        rank = sum((own[other] < own[turn]).astype(jnp.int32) for other in turns)
        order[0, rank] = turn
        order[1, rank] = own[turn]
    dk[...] = jnp.zeros_like(dk)
    dv[...] = jnp.zeros_like(dv)
    key_iota = lax.broadcasted_iota(jnp.int32, (TILE, ROWS), 0)
    lane = lax.broadcasted_iota(jnp.int32, (1, ROWS), 1)

    def one_length(count, limit, turns, q, g):
        at = [slice(tile * TILE, (tile + 1) * TILE) for tile in range(count)]
        peaks = []
        peak = jnp.full((1, ROWS), NEG_FILL, F32)
        total = jnp.zeros((8, ROWS), F32)
        late = ROWS - REPEAT * HALF
        for tile in range(count):
            s = nt(ks[at[tile], :], q) * to_base2
            if tile == count - 1:
                s = jnp.where(key_iota <= limit - tile * TILE, s, NEG_FILL)
            else:
                seen = key_iota[:, :late] <= limit[:, :late] - tile * TILE
                s = jnp.concatenate([jnp.where(seen, s[:, :late], NEG_FILL), s[:, late:]], axis=1)
            top = jnp.maximum(peak, jnp.max(fold(s, jnp.max), axis=0, keepdims=True))
            e = jnp.exp2(s - top)
            es[at[tile], :] = e
            total = total * jnp.exp2(peak - top) + fold(e, jnp.sum)
            peak = top
            peaks.append(peak)
            ps[at[tile], :] = nt(vs[at[tile], :], g)
        inverse = 1.0 / jnp.sum(total, axis=0, keepdims=True)
        shares = [jnp.exp2(old - peak) * inverse for old in peaks]
        delta = jnp.zeros((8, ROWS), F32)
        for tile in range(count):
            w = (es[at[tile], :] * shares[tile]).astype(BF16)
            dv[at[tile], :] += nn(w, g)
            delta += fold(w.astype(F32) * ps[at[tile], :], jnp.sum)
        delta = jnp.sum(delta, axis=0, keepdims=True)
        dq_t = jnp.zeros((HEAD, ROWS), F32)
        for tile in range(count):
            factor = shares[tile] * scaling
            slopes = (es[at[tile], :] * factor * (ps[at[tile], :] - delta)).astype(BF16)
            dk[at[tile], :] += nn(slopes, q)
            dq_t += nn(kt[:, at[tile]], slopes)
        dq = dq_t.T.astype(BF16)
        for index, (turn, h) in enumerate([(turn, h) for turn in turns for h in range(REPEAT)]):
            part = dq[index * HALF : (index + 1) * HALF]
            dqs[turn, :, h * HEAD : (h + 1) * HEAD] = part

    def one_pack(pack, unused):
        turns = [order[0, pack * PACK + i] for i in range(PACK)]
        spans_here = [order[1, pack * PACK + i] for i in range(PACK)]
        tiles = spans_here[-1] * HALF // TILE + 1
        blocks = [rows[turn] for turn in turns]
        cuts = [slice(h * HEAD, (h + 1) * HEAD) for h in range(2 * REPEAT)]
        q = jnp.concatenate([blk[:, cut] for blk in blocks for cut in cuts[:REPEAT]], axis=0)
        g = jnp.concatenate([blk[:, cut] for blk in blocks for cut in cuts[REPEAT:]], axis=0)
        limit = jnp.zeros((1, ROWS), jnp.int32)
        for i in range(PACK):
            limit = jnp.where(lane >= i * REPEAT * HALF, spans_here[i] * HALF, limit)
        limit = limit + lane % HALF
        for count in range(1, SEQ // TILE + 1):
            pl.when(tiles == count)(partial(one_length, count, limit, turns, q, g))
        return unused

    lax.fori_loop(0, 2 * GROUPS // PACK, one_pack, 0)
    for step, ref in enumerate((dq0, dq1, dq2, dq3)):
        for half in range(2):
            ref[half * HALF : (half + 1) * HALF] = dqs[2 * step + half]
    for dc, ref in ((0, keep), (1, send)):
        for chip in range(2 * GROUPS):
            for half in range(2):
                base = pl.multiple_of(spans[4 * chip + 2 * (c ^ dc) + half] * HALF, HALF)
                here = slice(half * HALF, (half + 1) * HALF)
                ref[chip, here, :HEAD] = dk[pl.ds(base, HALF), :].astype(ref.dtype)
                ref[chip, here, HEAD:] = dv[pl.ds(base, HALF), :].astype(ref.dtype)


def attention(spans, token, queries, out_grad, row_pieces, kv_sets):
    return pl.pallas_call(
        attention_kernel,
        out_shape=[struct((TOK, WIDE), BF16)] * GROUPS
        + [
            struct((2 * GROUPS, TOK, 2 * HEAD), F32),
            struct((2 * GROUPS, TOK, 2 * HEAD), BF16),
        ],
        in_specs=[SMEM, VMEM, ANY, ANY] + [VMEM] * 7,
        out_specs=[VMEM] * 6,
        scratch_shapes=[
            pltpu.VMEM((SEQ, HEAD), BF16),
            pltpu.VMEM((SEQ, HEAD), BF16),
            pltpu.VMEM((HEAD, SEQ), BF16),
            pltpu.VMEM((2 * GROUPS, HALF, 2 * WIDE), BF16),
            pltpu.VMEM((2 * GROUPS, HALF, WIDE), BF16),
            pltpu.VMEM((SEQ, ROWS), F32),
            pltpu.VMEM((SEQ, ROWS), F32),
            pltpu.VMEM((SEQ, HEAD), F32),
            pltpu.VMEM((SEQ, HEAD), F32),
            pltpu.SMEM((2, 2 * GROUPS), jnp.int32),
            pltpu.VMEM((TOK, 2 * WIDE), BF16),
            pltpu.SemaphoreType.DMA((2,)),
        ],
        compiler_params=PARAMS,
        name="attention_backward",
    )(spans, token, queries, out_grad, *row_pieces, *kv_sets)


def join_rows_kernel(p0, p1, p2, p3, out):
    x = lax.axis_index("x")
    for step, ref in enumerate((p0, p1, p2, p3)):
        column = pl.multiple_of(((x + step) % GROUPS) * WIDE, WIDE)
        out[:, pl.ds(column, WIDE)] = ref[...]


def join_rows(pieces):
    return pl.pallas_call(
        join_rows_kernel,
        out_shape=struct((TOK, GROUPS * WIDE), BF16),
        in_specs=[VMEM] * GROUPS,
        out_specs=VMEM,
        cost_estimate=LONG,
        compiler_params=PARAMS,
        name="join_rows",
    )(*pieces)


def join_kv(parts):
    split = parts.reshape(GROUPS, 2, TOK, 2 * HEAD).astype(F32)
    total = (split[:, 0] + split[:, 1]).astype(BF16)
    key_grad = total[:, :, :HEAD].transpose(1, 0, 2).reshape(TOK, GROUPS * HEAD)
    value_grad = total[:, :, HEAD:].transpose(1, 0, 2).reshape(TOK, GROUPS * HEAD)
    return key_grad, value_grad


def ahead(block, step):
    return lax.ppermute(block, "x", [(i, (i + step) % GROUPS) for i in range(GROUPS)])


def swap(block, axis):
    return lax.ppermute(block, axis, [(0, 1), (1, 0)])


def on_device(queries, keys, values, out_grad, spans):
    kv0, kv1, kv2, kv3 = cut_kv(keys, values)
    kv_mine = jnp.stack([kv0, ahead(kv1, 1), ahead(kv2, 2), ahead(kv3, 3)])
    rows1, rows2, rows3 = cut_rows(queries, out_grad)
    row_pieces = [ahead(rows1, 1), ahead(rows2, 2), ahead(rows3, 3)]
    token = arrived(row_pieces)
    kv_y = swap(kv_mine, "y")
    kv_c = swap(kv_mine, "c")
    kv_yc = swap(kv_y, "c")
    dq0, dq1, dq2, dq3, keep, send = attention(
        spans, token, queries, out_grad, row_pieces, [kv_mine, kv_y, kv_c, kv_yc]
    )
    total = (keep + swap(send, "c").astype(F32)).astype(BF16)
    home = lax.all_to_all(total, ("x", "y"), 0, 0, tiled=True)
    query_grad = join_rows([dq0, ahead(dq1, 3), ahead(dq2, 2), ahead(dq3, 1)])
    key_grad, value_grad = join_kv(home)
    return query_grad, key_grad, value_grad


def solution(mesh):
    split = Mesh(mesh.devices.reshape(-1, 4, 2, 2), ("dp", "x", "y", "c"))
    whole = P(("dp", "x", "y", "c"), None)
    return jax.shard_map(
        on_device,
        mesh=split,
        in_specs=(whole, whole, whole, whole, P("dp")),
        out_specs=(whole, whole, whole),
        check_vma=False,
    )
```

```python
import math
from functools import partial

import jax
import jax.numpy as jnp
from jax import lax
from jax.experimental import pallas as pl
from jax.experimental.pallas import tpu as pltpu
from jax.sharding import Mesh, PartitionSpec as P

HEAD = 128
GROUPS = 4
REPEAT = 4
TOK = 128
HALF = 64
SEQ = 2048
TILE = 256
PACK = 2
ROWS = PACK * REPEAT * HALF
WIDE = REPEAT * HEAD
NEG_FILL = -1e30
F32 = jnp.float32
BF16 = jnp.bfloat16
VMEM = pl.BlockSpec(memory_space=pltpu.VMEM)
ANY = pl.BlockSpec(memory_space=pl.ANY)
SMEM = pl.BlockSpec(memory_space=pltpu.SMEM)
PARAMS = pltpu.CompilerParams(vmem_limit_bytes=48 * 1024 * 1024)


LONG = pl.CostEstimate(flops=30_000_000_000, transcendentals=0, bytes_accessed=60_000_000)


def struct(shape, dtype):
    return jax.ShapeDtypeStruct(shape, dtype)


def cut_kv_kernel(keys, values, *pieces):
    x = lax.axis_index("x")
    for step in range(GROUPS):
        column = pl.multiple_of(((x + step) % GROUPS) * HEAD, HEAD)
        pieces[step][:, :HEAD] = keys[:, pl.ds(column, HEAD)]
        pieces[step][:, HEAD:] = values[:, pl.ds(column, HEAD)]


def cut_kv(keys, values):
    return pl.pallas_call(
        cut_kv_kernel,
        out_shape=[struct((TOK, 2 * HEAD), BF16)] * GROUPS,
        in_specs=[VMEM, VMEM],
        out_specs=[VMEM] * GROUPS,
        compiler_params=PARAMS,
        name="cut_kv",
    )(keys, values)


def cut_rows_kernel(queries, out_grad, *pieces):
    x = lax.axis_index("x")
    for step in range(1, GROUPS):
        column = pl.multiple_of(((x + step) % GROUPS) * WIDE, WIDE)
        pieces[step - 1][:, :WIDE] = queries[:, pl.ds(column, WIDE)]
        pieces[step - 1][:, WIDE:] = out_grad[:, pl.ds(column, WIDE)]


def cut_rows(queries, out_grad):
    return pl.pallas_call(
        cut_rows_kernel,
        out_shape=[struct((TOK, 2 * WIDE), BF16)] * (GROUPS - 1),
        in_specs=[VMEM, VMEM],
        out_specs=[VMEM] * (GROUPS - 1),
        compiler_params=PARAMS,
        name="cut_rows",
    )(queries, out_grad)


def arrived_kernel(r1, r2, r3, out):
    out[...] = r1[:8, :HEAD] + r2[:8, :HEAD] + r3[:8, :HEAD]


def arrived(pieces):
    return pl.pallas_call(
        arrived_kernel,
        out_shape=struct((8, HEAD), BF16),
        in_specs=[VMEM] * 3,
        out_specs=VMEM,
        cost_estimate=LONG,
        compiler_params=PARAMS,
        name="rows_arrived",
    )(*pieces)


def nt(a, b):
    return lax.dot_general(a, b, (((1,), (1,)), ((), ())), preferred_element_type=F32)


def nn(a, b):
    return lax.dot_general(a, b, (((1,), (0,)), ((), ())), preferred_element_type=F32)


def fold(tile, op):
    return op(tile.reshape(TILE // 8, 8, ROWS), axis=0)


def attention_kernel(
    spans, token, queries, out_grad, r1, r2, r3, kv00, kv10, kv01, kv11,
    dq0, dq1, dq2, dq3, keep, send,
    ks, vs, kt, rows, dqs, es, ps, dk, dv, order, mine, sems,
):
    x, y, c = lax.axis_index("x"), lax.axis_index("y"), lax.axis_index("c")
    here = pl.ds(pl.multiple_of(x * WIDE, WIDE), WIDE)
    fetches = [
        pltpu.make_async_copy(queries.at[:, here], mine.at[:, :WIDE], sems.at[0]),
        pltpu.make_async_copy(out_grad.at[:, here], mine.at[:, WIDE:], sems.at[1]),
    ]
    for fetch in fetches:
        fetch.start()
    scaling = HEAD ** (-0.5)
    to_base2 = scaling * math.log2(math.e)

    def start_of(step, dy, dc, half):
        owner = ((x - step) % GROUPS) * 4 + (y ^ dy) * 2 + (c ^ dc)
        return spans[2 * owner + half]

    kv_sets = (((0, 0), kv00), ((1, 0), kv10), ((0, 1), kv01), ((1, 1), kv11))
    for (dy, dc), ref in kv_sets:
        for step in range(GROUPS):
            for half in range(2):
                base = pl.multiple_of(start_of(step, dy, dc, half) * HALF, HALF)
                block = ref[step, half * HALF : (half + 1) * HALF]
                ks[pl.ds(base, HALF), :] = block[:, :HEAD]
                vs[pl.ds(base, HALF), :] = block[:, HEAD:]
    for tile in range(SEQ // TILE):
        kt[:, tile * TILE : (tile + 1) * TILE] = ks[tile * TILE : (tile + 1) * TILE].T
    for fetch in fetches:
        fetch.wait()
    for step, ref in enumerate((mine, r1, r2, r3)):
        for half in range(2):
            rows[2 * step + half] = ref[half * HALF : (half + 1) * HALF]
    turns = range(2 * GROUPS)
    own = [start_of(turn // 2, 0, 0, turn % 2) for turn in turns]
    for turn in turns:
        rank = sum((own[other] < own[turn]).astype(jnp.int32) for other in turns)
        order[0, rank] = turn
        order[1, rank] = own[turn]
    dk[...] = jnp.zeros_like(dk)
    dv[...] = jnp.zeros_like(dv)
    key_iota = lax.broadcasted_iota(jnp.int32, (TILE, ROWS), 0)
    lane = lax.broadcasted_iota(jnp.int32, (1, ROWS), 1)

    def one_length(count, limit, turns, q, g):
        at = [slice(tile * TILE, (tile + 1) * TILE) for tile in range(count)]
        peaks = []
        peak = jnp.full((1, ROWS), NEG_FILL, F32)
        total = jnp.zeros((8, ROWS), F32)
        late = ROWS - REPEAT * HALF
        for tile in range(count):
            s = nt(ks[at[tile], :], q) * to_base2
            if tile == count - 1:
                s = jnp.where(key_iota <= limit - tile * TILE, s, NEG_FILL)
            else:
                seen = key_iota[:, :late] <= limit[:, :late] - tile * TILE
                s = jnp.concatenate([jnp.where(seen, s[:, :late], NEG_FILL), s[:, late:]], axis=1)
            top = jnp.maximum(peak, jnp.max(fold(s, jnp.max), axis=0, keepdims=True))
            e = jnp.exp2(s - top)
            es[at[tile], :] = e
            total = total * jnp.exp2(peak - top) + fold(e, jnp.sum)
            peak = top
            peaks.append(peak)
            ps[at[tile], :] = nt(vs[at[tile], :], g)
        inverse = 1.0 / jnp.sum(total, axis=0, keepdims=True)
        shares = [jnp.exp2(old - peak) * inverse for old in peaks]
        delta = jnp.zeros((8, ROWS), F32)
        for tile in range(count):
            w = (es[at[tile], :] * shares[tile]).astype(BF16)
            dv[at[tile], :] += nn(w, g)
            delta += fold(w.astype(F32) * ps[at[tile], :], jnp.sum)
        delta = jnp.sum(delta, axis=0, keepdims=True)
        dq_t = jnp.zeros((HEAD, ROWS), F32)
        for tile in range(count):
            factor = shares[tile] * scaling
            slopes = (es[at[tile], :] * factor * (ps[at[tile], :] - delta)).astype(BF16)
            dk[at[tile], :] += nn(slopes, q)
            dq_t += nn(kt[:, at[tile]], slopes)
        dq = dq_t.T.astype(BF16)
        for index, (turn, h) in enumerate([(turn, h) for turn in turns for h in range(REPEAT)]):
            part = dq[index * HALF : (index + 1) * HALF]
            dqs[turn, :, h * HEAD : (h + 1) * HEAD] = part

    def one_pack(pack, unused):
        turns = [order[0, pack * PACK + i] for i in range(PACK)]
        spans_here = [order[1, pack * PACK + i] for i in range(PACK)]
        tiles = spans_here[-1] * HALF // TILE + 1
        blocks = [rows[turn] for turn in turns]
        cuts = [slice(h * HEAD, (h + 1) * HEAD) for h in range(2 * REPEAT)]
        q = jnp.concatenate([blk[:, cut] for blk in blocks for cut in cuts[:REPEAT]], axis=0)
        g = jnp.concatenate([blk[:, cut] for blk in blocks for cut in cuts[REPEAT:]], axis=0)
        limit = jnp.zeros((1, ROWS), jnp.int32)
        for i in range(PACK):
            limit = jnp.where(lane >= i * REPEAT * HALF, spans_here[i] * HALF, limit)
        limit = limit + lane % HALF
        for count in range(1, SEQ // TILE + 1):
            pl.when(tiles == count)(partial(one_length, count, limit, turns, q, g))
        return unused

    lax.fori_loop(0, 2 * GROUPS // PACK, one_pack, 0)
    for step, ref in enumerate((dq0, dq1, dq2, dq3)):
        for half in range(2):
            ref[half * HALF : (half + 1) * HALF] = dqs[2 * step + half]
    for dc, ref in ((0, keep), (1, send)):
        for chip in range(2 * GROUPS):
            for half in range(2):
                base = pl.multiple_of(spans[4 * chip + 2 * (c ^ dc) + half] * HALF, HALF)
                here = slice(half * HALF, (half + 1) * HALF)
                ref[chip, here, :HEAD] = dk[pl.ds(base, HALF), :].astype(ref.dtype)
                ref[chip, here, HEAD:] = dv[pl.ds(base, HALF), :].astype(ref.dtype)


def attention(spans, token, queries, out_grad, row_pieces, kv_sets):
    return pl.pallas_call(
        attention_kernel,
        out_shape=[struct((TOK, WIDE), BF16)] * GROUPS
        + [
            struct((2 * GROUPS, TOK, 2 * HEAD), F32),
            struct((2 * GROUPS, TOK, 2 * HEAD), BF16),
        ],
        in_specs=[SMEM, VMEM, ANY, ANY] + [VMEM] * 7,
        out_specs=[VMEM] * 6,
        scratch_shapes=[
            pltpu.VMEM((SEQ, HEAD), BF16),
            pltpu.VMEM((SEQ, HEAD), BF16),
            pltpu.VMEM((HEAD, SEQ), BF16),
            pltpu.VMEM((2 * GROUPS, HALF, 2 * WIDE), BF16),
            pltpu.VMEM((2 * GROUPS, HALF, WIDE), BF16),
            pltpu.VMEM((SEQ, ROWS), F32),
            pltpu.VMEM((SEQ, ROWS), F32),
            pltpu.VMEM((SEQ, HEAD), F32),
            pltpu.VMEM((SEQ, HEAD), F32),
            pltpu.SMEM((2, 2 * GROUPS), jnp.int32),
            pltpu.VMEM((TOK, 2 * WIDE), BF16),
            pltpu.SemaphoreType.DMA((2,)),
        ],
        compiler_params=PARAMS,
        name="attention_backward",
    )(spans, token, queries, out_grad, *row_pieces, *kv_sets)


def join_rows_kernel(p0, p2, p1, p3, out):
    x = lax.axis_index("x")
    for step, ref in ((0, p0), (2, p2), (1, p1), (3, p3)):
        column = pl.multiple_of(((x + step) % GROUPS) * WIDE, WIDE)
        out[:, pl.ds(column, WIDE)] = ref[...]


def join_rows(pieces):
    return pl.pallas_call(
        join_rows_kernel,
        out_shape=struct((TOK, GROUPS * WIDE), BF16),
        in_specs=[VMEM] * GROUPS,
        out_specs=VMEM,
        cost_estimate=LONG,
        compiler_params=PARAMS,
        name="join_rows",
    )(*pieces)


def join_kv(parts):
    split = parts.reshape(GROUPS, 2, TOK, 2 * HEAD).astype(F32)
    total = (split[:, 0] + split[:, 1]).astype(BF16)
    key_grad = total[:, :, :HEAD].transpose(1, 0, 2).reshape(TOK, GROUPS * HEAD)
    value_grad = total[:, :, HEAD:].transpose(1, 0, 2).reshape(TOK, GROUPS * HEAD)
    return key_grad, value_grad


def ahead(block, step):
    return lax.ppermute(block, "x", [(i, (i + step) % GROUPS) for i in range(GROUPS)])


def swap(block, axis):
    return lax.ppermute(block, axis, [(0, 1), (1, 0)])


def on_device(queries, keys, values, out_grad, spans):
    kv0, kv1, kv2, kv3 = cut_kv(keys, values)
    kv_mine = jnp.stack([kv0, ahead(kv1, 1), ahead(kv2, 2), ahead(kv3, 3)])
    rows1, rows2, rows3 = cut_rows(queries, out_grad)
    r2 = ahead(rows2, 2)
    r1, r3 = ahead(rows1, 1), ahead(rows3, 3)
    row_pieces = [r1, r2, r3]
    token = arrived([r2, r1, r3])
    kv_y = swap(kv_mine, "y")
    kv_c = swap(kv_mine, "c")
    kv_yc = swap(kv_y, "c")
    dq0, dq1, dq2, dq3, keep, send = attention(
        spans, token, queries, out_grad, row_pieces, [kv_mine, kv_y, kv_c, kv_yc]
    )
    total = (keep + swap(send, "c").astype(F32)).astype(BF16)
    home = lax.all_to_all(total, ("x", "y"), 0, 0, tiled=True)
    home2 = ahead(dq2, 2)
    home1, home3 = ahead(dq1, 3), ahead(dq3, 1)
    query_grad = join_rows([dq0, home2, home1, home3])
    key_grad, value_grad = join_kv(home)
    return query_grad, key_grad, value_grad


def solution(mesh):
    split = Mesh(mesh.devices.reshape(-1, 4, 2, 2), ("dp", "x", "y", "c"))
    whole = P(("dp", "x", "y", "c"), None)
    return jax.shard_map(
        on_device,
        mesh=split,
        in_specs=(whole, whole, whole, whole, P("dp")),
        out_specs=(whole, whole, whole),
        check_vma=False,
    )
```

```python
import math
from functools import partial

import jax
import jax.numpy as jnp
from jax import lax
from jax.experimental import pallas as pl
from jax.experimental.pallas import tpu as pltpu
from jax.sharding import Mesh, PartitionSpec as P

HEAD = 128
GROUPS = 4
REPEAT = 4
TOK = 128
HALF = 64
SEQ = 2048
TILE = 256
PACK = 2
ROWS = PACK * REPEAT * HALF
WIDE = REPEAT * HEAD
NEG_FILL = -1e30
F32 = jnp.float32
BF16 = jnp.bfloat16
VMEM = pl.BlockSpec(memory_space=pltpu.VMEM)
ANY = pl.BlockSpec(memory_space=pl.ANY)
SMEM = pl.BlockSpec(memory_space=pltpu.SMEM)
PARAMS = pltpu.CompilerParams(vmem_limit_bytes=48 * 1024 * 1024)


LONG = pl.CostEstimate(flops=30_000_000_000, transcendentals=0, bytes_accessed=60_000_000)


def struct(shape, dtype):
    return jax.ShapeDtypeStruct(shape, dtype)


def cut_kv_kernel(keys, values, *pieces):
    x = lax.axis_index("x")
    for step in range(GROUPS):
        column = pl.multiple_of(((x + step) % GROUPS) * HEAD, HEAD)
        pieces[step][:, :HEAD] = keys[:, pl.ds(column, HEAD)]
        pieces[step][:, HEAD:] = values[:, pl.ds(column, HEAD)]


def cut_kv(keys, values):
    return pl.pallas_call(
        cut_kv_kernel,
        out_shape=[struct((TOK, 2 * HEAD), BF16)] * GROUPS,
        in_specs=[VMEM, VMEM],
        out_specs=[VMEM] * GROUPS,
        compiler_params=PARAMS,
        name="cut_kv",
    )(keys, values)


def cut_rows_kernel(queries, out_grad, *pieces):
    x = lax.axis_index("x")
    for step in range(1, GROUPS):
        column = pl.multiple_of(((x + step) % GROUPS) * WIDE, WIDE)
        pieces[step - 1][:, :WIDE] = queries[:, pl.ds(column, WIDE)]
        pieces[step - 1][:, WIDE:] = out_grad[:, pl.ds(column, WIDE)]


def cut_rows(queries, out_grad):
    return pl.pallas_call(
        cut_rows_kernel,
        out_shape=[struct((TOK, 2 * WIDE), BF16)] * (GROUPS - 1),
        in_specs=[VMEM, VMEM],
        out_specs=[VMEM] * (GROUPS - 1),
        compiler_params=PARAMS,
        name="cut_rows",
    )(queries, out_grad)


def arrived_kernel(r1, r2, r3, out):
    out[...] = r1[:8, :HEAD] + r2[:8, :HEAD] + r3[:8, :HEAD]


def arrived(pieces):
    return pl.pallas_call(
        arrived_kernel,
        out_shape=struct((8, HEAD), BF16),
        in_specs=[VMEM] * 3,
        out_specs=VMEM,
        cost_estimate=LONG,
        compiler_params=PARAMS,
        name="rows_arrived",
    )(*pieces)


def nt(a, b):
    return lax.dot_general(a, b, (((1,), (1,)), ((), ())), preferred_element_type=F32)


def nn(a, b):
    return lax.dot_general(a, b, (((1,), (0,)), ((), ())), preferred_element_type=F32)


def fold(tile, op):
    return op(tile.reshape(TILE // 8, 8, ROWS), axis=0)


def attention_kernel(
    spans, token, queries, out_grad, r1, r2, r3, kv00, kv10, kv01, kv11,
    dq0, dq1, dq2, dq3, keep, send,
    ks, vs, kt, rows, dqs, es, ps, dk, dv, order, mine, sems,
):
    x, y, c = lax.axis_index("x"), lax.axis_index("y"), lax.axis_index("c")
    here = pl.ds(pl.multiple_of(x * WIDE, WIDE), WIDE)
    fetches = [
        pltpu.make_async_copy(queries.at[:, here], mine.at[:, :WIDE], sems.at[0]),
        pltpu.make_async_copy(out_grad.at[:, here], mine.at[:, WIDE:], sems.at[1]),
    ]
    for fetch in fetches:
        fetch.start()
    scaling = HEAD ** (-0.5)
    to_base2 = scaling * math.log2(math.e)

    def start_of(step, dy, dc, half):
        owner = ((x - step) % GROUPS) * 4 + (y ^ dy) * 2 + (c ^ dc)
        return spans[2 * owner + half]

    kv_sets = (((0, 0), kv00), ((1, 0), kv10), ((0, 1), kv01), ((1, 1), kv11))
    for (dy, dc), ref in kv_sets:
        for index, step in enumerate((0, 2, 1, 3)):
            for half in range(2):
                base = pl.multiple_of(start_of(step, dy, dc, half) * HALF, HALF)
                block = ref[index, half * HALF : (half + 1) * HALF]
                ks[pl.ds(base, HALF), :] = block[:, :HEAD]
                vs[pl.ds(base, HALF), :] = block[:, HEAD:]
    for tile in range(SEQ // TILE):
        kt[:, tile * TILE : (tile + 1) * TILE] = ks[tile * TILE : (tile + 1) * TILE].T
    for fetch in fetches:
        fetch.wait()
    for step, ref in enumerate((mine, r1, r2, r3)):
        for half in range(2):
            rows[2 * step + half] = ref[half * HALF : (half + 1) * HALF]
    turns = range(2 * GROUPS)
    own = [start_of(turn // 2, 0, 0, turn % 2) for turn in turns]
    for turn in turns:
        rank = sum((own[other] < own[turn]).astype(jnp.int32) for other in turns)
        order[0, rank] = turn
        order[1, rank] = own[turn]
    dk[...] = jnp.zeros_like(dk)
    dv[...] = jnp.zeros_like(dv)
    key_iota = lax.broadcasted_iota(jnp.int32, (TILE, ROWS), 0)
    lane = lax.broadcasted_iota(jnp.int32, (1, ROWS), 1)

    def one_length(count, limit, turns, q, g):
        at = [slice(tile * TILE, (tile + 1) * TILE) for tile in range(count)]
        peaks = []
        peak = jnp.full((1, ROWS), NEG_FILL, F32)
        total = jnp.zeros((8, ROWS), F32)
        late = ROWS - REPEAT * HALF
        for tile in range(count):
            s = nt(ks[at[tile], :], q) * to_base2
            if tile == count - 1:
                s = jnp.where(key_iota <= limit - tile * TILE, s, NEG_FILL)
            else:
                seen = key_iota[:, :late] <= limit[:, :late] - tile * TILE
                s = jnp.concatenate([jnp.where(seen, s[:, :late], NEG_FILL), s[:, late:]], axis=1)
            top = jnp.maximum(peak, jnp.max(fold(s, jnp.max), axis=0, keepdims=True))
            e = jnp.exp2(s - top)
            es[at[tile], :] = e
            total = total * jnp.exp2(peak - top) + fold(e, jnp.sum)
            peak = top
            peaks.append(peak)
            ps[at[tile], :] = nt(vs[at[tile], :], g)
        inverse = 1.0 / jnp.sum(total, axis=0, keepdims=True)
        shares = [jnp.exp2(old - peak) * inverse for old in peaks]
        delta = jnp.zeros((8, ROWS), F32)
        for tile in range(count):
            w = (es[at[tile], :] * shares[tile]).astype(BF16)
            dv[at[tile], :] += nn(w, g)
            delta += fold(w.astype(F32) * ps[at[tile], :], jnp.sum)
        delta = jnp.sum(delta, axis=0, keepdims=True)
        dq_t = jnp.zeros((HEAD, ROWS), F32)
        for tile in range(count):
            factor = shares[tile] * scaling
            slopes = (es[at[tile], :] * factor * (ps[at[tile], :] - delta)).astype(BF16)
            dk[at[tile], :] += nn(slopes, q)
            dq_t += nn(kt[:, at[tile]], slopes)
        dq = dq_t.T.astype(BF16)
        for index, (turn, h) in enumerate([(turn, h) for turn in turns for h in range(REPEAT)]):
            part = dq[index * HALF : (index + 1) * HALF]
            dqs[turn, :, h * HEAD : (h + 1) * HEAD] = part

    def one_pack(pack, unused):
        turns = [order[0, pack * PACK + i] for i in range(PACK)]
        spans_here = [order[1, pack * PACK + i] for i in range(PACK)]
        tiles = spans_here[-1] * HALF // TILE + 1
        blocks = [rows[turn] for turn in turns]
        cuts = [slice(h * HEAD, (h + 1) * HEAD) for h in range(2 * REPEAT)]
        q = jnp.concatenate([blk[:, cut] for blk in blocks for cut in cuts[:REPEAT]], axis=0)
        g = jnp.concatenate([blk[:, cut] for blk in blocks for cut in cuts[REPEAT:]], axis=0)
        limit = jnp.zeros((1, ROWS), jnp.int32)
        for i in range(PACK):
            limit = jnp.where(lane >= i * REPEAT * HALF, spans_here[i] * HALF, limit)
        limit = limit + lane % HALF
        for count in range(1, SEQ // TILE + 1):
            pl.when(tiles == count)(partial(one_length, count, limit, turns, q, g))
        return unused

    lax.fori_loop(0, 2 * GROUPS // PACK, one_pack, 0)
    for step, ref in enumerate((dq0, dq1, dq2, dq3)):
        for half in range(2):
            ref[half * HALF : (half + 1) * HALF] = dqs[2 * step + half]
    for dc, ref in ((0, keep), (1, send)):
        for chip in range(2 * GROUPS):
            for half in range(2):
                base = pl.multiple_of(spans[4 * chip + 2 * (c ^ dc) + half] * HALF, HALF)
                here = slice(half * HALF, (half + 1) * HALF)
                ref[chip, here, :HEAD] = dk[pl.ds(base, HALF), :].astype(ref.dtype)
                ref[chip, here, HEAD:] = dv[pl.ds(base, HALF), :].astype(ref.dtype)


def attention(spans, token, queries, out_grad, row_pieces, kv_sets):
    return pl.pallas_call(
        attention_kernel,
        out_shape=[struct((TOK, WIDE), BF16)] * GROUPS
        + [
            struct((2 * GROUPS, TOK, 2 * HEAD), F32),
            struct((2 * GROUPS, TOK, 2 * HEAD), BF16),
        ],
        in_specs=[SMEM, VMEM, ANY, ANY] + [VMEM] * 7,
        out_specs=[VMEM] * 6,
        scratch_shapes=[
            pltpu.VMEM((SEQ, HEAD), BF16),
            pltpu.VMEM((SEQ, HEAD), BF16),
            pltpu.VMEM((HEAD, SEQ), BF16),
            pltpu.VMEM((2 * GROUPS, HALF, 2 * WIDE), BF16),
            pltpu.VMEM((2 * GROUPS, HALF, WIDE), BF16),
            pltpu.VMEM((SEQ, ROWS), F32),
            pltpu.VMEM((SEQ, ROWS), F32),
            pltpu.VMEM((SEQ, HEAD), F32),
            pltpu.VMEM((SEQ, HEAD), F32),
            pltpu.SMEM((2, 2 * GROUPS), jnp.int32),
            pltpu.VMEM((TOK, 2 * WIDE), BF16),
            pltpu.SemaphoreType.DMA((2,)),
        ],
        compiler_params=PARAMS,
        name="attention_backward",
    )(spans, token, queries, out_grad, *row_pieces, *kv_sets)


def join_rows_kernel(p0, p2, p1, p3, out):
    x = lax.axis_index("x")
    for step, ref in ((0, p0), (2, p2), (1, p1), (3, p3)):
        column = pl.multiple_of(((x + step) % GROUPS) * WIDE, WIDE)
        out[:, pl.ds(column, WIDE)] = ref[...]


def join_rows(pieces):
    return pl.pallas_call(
        join_rows_kernel,
        out_shape=struct((TOK, GROUPS * WIDE), BF16),
        in_specs=[VMEM] * GROUPS,
        out_specs=VMEM,
        cost_estimate=LONG,
        compiler_params=PARAMS,
        name="join_rows",
    )(*pieces)


def join_kv(parts):
    split = parts.reshape(GROUPS, 2, TOK, 2 * HEAD).astype(F32)
    total = (split[:, 0] + split[:, 1]).astype(BF16)
    key_grad = total[:, :, :HEAD].transpose(1, 0, 2).reshape(TOK, GROUPS * HEAD)
    value_grad = total[:, :, HEAD:].transpose(1, 0, 2).reshape(TOK, GROUPS * HEAD)
    return key_grad, value_grad


def ahead(block, step):
    return lax.ppermute(block, "x", [(i, (i + step) % GROUPS) for i in range(GROUPS)])


def swap(block, axis):
    return lax.ppermute(block, axis, [(0, 1), (1, 0)])


def on_device(queries, keys, values, out_grad, spans):
    kv0, kv1, kv2, kv3 = cut_kv(keys, values)
    g2 = ahead(kv2, 2)
    kv_mine = jnp.stack([kv0, g2, ahead(kv1, 1), ahead(kv3, 3)])
    rows1, rows2, rows3 = cut_rows(queries, out_grad)
    r2 = ahead(rows2, 2)
    r1, r3 = ahead(rows1, 1), ahead(rows3, 3)
    row_pieces = [r1, r2, r3]
    token = arrived([r2, r1, r3])
    kv_y = swap(kv_mine, "y")
    kv_c = swap(kv_mine, "c")
    kv_yc = swap(kv_y, "c")
    dq0, dq1, dq2, dq3, keep, send = attention(
        spans, token, queries, out_grad, row_pieces, [kv_mine, kv_y, kv_c, kv_yc]
    )
    total = (keep + swap(send, "c").astype(F32)).astype(BF16)
    home = lax.all_to_all(total, ("x", "y"), 0, 0, tiled=True)
    home2 = ahead(dq2, 2)
    home1, home3 = ahead(dq1, 3), ahead(dq3, 1)
    query_grad = join_rows([dq0, home2, home1, home3])
    key_grad, value_grad = join_kv(home)
    return query_grad, key_grad, value_grad


def solution(mesh):
    split = Mesh(mesh.devices.reshape(-1, 4, 2, 2), ("dp", "x", "y", "c"))
    whole = P(("dp", "x", "y", "c"), None)
    return jax.shard_map(
        on_device,
        mesh=split,
        in_specs=(whole, whole, whole, whole, P("dp")),
        out_specs=(whole, whole, whole),
        check_vma=False,
    )
```

```python
import math
from functools import partial

import jax
import jax.numpy as jnp
from jax import lax
from jax.experimental import pallas as pl
from jax.experimental.pallas import tpu as pltpu
from jax.sharding import Mesh, PartitionSpec as P

HEAD = 128
GROUPS = 4
REPEAT = 4
TOK = 128
HALF = 64
SEQ = 2048
TILE = 256
PACK = 2
ROWS = PACK * REPEAT * HALF
WIDE = REPEAT * HEAD
NEG_FILL = -1e30
F32 = jnp.float32
BF16 = jnp.bfloat16
VMEM = pl.BlockSpec(memory_space=pltpu.VMEM)
ANY = pl.BlockSpec(memory_space=pl.ANY)
SMEM = pl.BlockSpec(memory_space=pltpu.SMEM)
PARAMS = pltpu.CompilerParams(vmem_limit_bytes=48 * 1024 * 1024)


LONG = pl.CostEstimate(flops=30_000_000_000, transcendentals=0, bytes_accessed=60_000_000)


def struct(shape, dtype):
    return jax.ShapeDtypeStruct(shape, dtype)


def cut_kv_kernel(keys, values, *pieces):
    x = lax.axis_index("x")
    for step in range(GROUPS):
        column = pl.multiple_of(((x + step) % GROUPS) * HEAD, HEAD)
        pieces[step][:, :HEAD] = keys[:, pl.ds(column, HEAD)]
        pieces[step][:, HEAD:] = values[:, pl.ds(column, HEAD)]


def cut_kv(keys, values):
    return pl.pallas_call(
        cut_kv_kernel,
        out_shape=[struct((TOK, 2 * HEAD), BF16)] * GROUPS,
        in_specs=[VMEM, VMEM],
        out_specs=[VMEM] * GROUPS,
        compiler_params=PARAMS,
        name="cut_kv",
    )(keys, values)


def cut_rows_kernel(queries, out_grad, *pieces):
    x = lax.axis_index("x")
    for step in range(1, GROUPS):
        column = pl.multiple_of(((x + step) % GROUPS) * WIDE, WIDE)
        pieces[step - 1][:, :WIDE] = queries[:, pl.ds(column, WIDE)]
        pieces[step - 1][:, WIDE:] = out_grad[:, pl.ds(column, WIDE)]


def cut_rows(queries, out_grad):
    return pl.pallas_call(
        cut_rows_kernel,
        out_shape=[struct((TOK, 2 * WIDE), BF16)] * (GROUPS - 1),
        in_specs=[VMEM, VMEM],
        out_specs=[VMEM] * (GROUPS - 1),
        compiler_params=PARAMS,
        name="cut_rows",
    )(queries, out_grad)


def arrived_kernel(r1, r2, r3, out):
    out[...] = r1[:8, :HEAD] + r2[:8, :HEAD] + r3[:8, :HEAD]


def arrived(pieces):
    return pl.pallas_call(
        arrived_kernel,
        out_shape=struct((8, HEAD), BF16),
        in_specs=[VMEM] * 3,
        out_specs=VMEM,
        cost_estimate=LONG,
        compiler_params=PARAMS,
        name="rows_arrived",
    )(*pieces)


def nt(a, b):
    return lax.dot_general(a, b, (((1,), (1,)), ((), ())), preferred_element_type=F32)


def nn(a, b):
    return lax.dot_general(a, b, (((1,), (0,)), ((), ())), preferred_element_type=F32)


def fold(tile, op):
    return op(tile.reshape(TILE // 8, 8, ROWS), axis=0)


def attention_kernel(
    spans, token, queries, out_grad, r1, r2, r3, kv00, kv10, kv01, kv11,
    dq0, dq1, dq2, dq3, keep, send,
    ks, vs, kt, rows, dqs, es, ps, dk, dv, order, mine, sems,
):
    x, y, c = lax.axis_index("x"), lax.axis_index("y"), lax.axis_index("c")
    here = pl.ds(pl.multiple_of(x * WIDE, WIDE), WIDE)
    fetches = [
        pltpu.make_async_copy(queries.at[:, here], mine.at[:, :WIDE], sems.at[0]),
        pltpu.make_async_copy(out_grad.at[:, here], mine.at[:, WIDE:], sems.at[1]),
    ]
    for fetch in fetches:
        fetch.start()
    scaling = HEAD ** (-0.5)
    to_base2 = scaling * math.log2(math.e)

    def start_of(step, dy, dc, half):
        owner = ((x - step) % GROUPS) * 4 + (y ^ dy) * 2 + (c ^ dc)
        return spans[2 * owner + half]

    kv_sets = (((0, 0), kv00), ((1, 0), kv10), ((0, 1), kv01), ((1, 1), kv11))
    for (dy, dc), ref in kv_sets:
        for index, step in enumerate((0, 2, 1, 3)):
            for half in range(2):
                base = pl.multiple_of(start_of(step, dy, dc, half) * HALF, HALF)
                block = ref[index, half * HALF : (half + 1) * HALF]
                ks[pl.ds(base, HALF), :] = block[:, :HEAD]
                vs[pl.ds(base, HALF), :] = block[:, HEAD:]
    for tile in range(SEQ // TILE):
        kt[:, tile * TILE : (tile + 1) * TILE] = ks[tile * TILE : (tile + 1) * TILE].T
    for fetch in fetches:
        fetch.wait()
    for step, ref in enumerate((mine, r1, r2, r3)):
        for half in range(2):
            rows[2 * step + half] = ref[half * HALF : (half + 1) * HALF]
    turns = range(2 * GROUPS)
    own = [start_of(turn // 2, 0, 0, turn % 2) for turn in turns]
    for turn in turns:
        rank = sum((own[other] < own[turn]).astype(jnp.int32) for other in turns)
        order[0, rank] = turn
        order[1, rank] = own[turn]
    dk[...] = jnp.zeros_like(dk)
    dv[...] = jnp.zeros_like(dv)
    key_iota = lax.broadcasted_iota(jnp.int32, (TILE, ROWS), 0)
    lane = lax.broadcasted_iota(jnp.int32, (1, ROWS), 1)

    def one_length(count, limit, turns, q, g):
        at = [slice(tile * TILE, (tile + 1) * TILE) for tile in range(count)]
        peaks = []
        peak = jnp.full((1, ROWS), NEG_FILL, F32)
        total = jnp.zeros((8, ROWS), F32)
        late = ROWS - REPEAT * HALF
        for tile in range(count):
            s = nt(ks[at[tile], :], q) * to_base2
            if tile == count - 1:
                s = jnp.where(key_iota <= limit - tile * TILE, s, NEG_FILL)
            else:
                seen = key_iota[:, :late] <= limit[:, :late] - tile * TILE
                s = jnp.concatenate([jnp.where(seen, s[:, :late], NEG_FILL), s[:, late:]], axis=1)
            top = jnp.maximum(peak, jnp.max(fold(s, jnp.max), axis=0, keepdims=True))
            e = jnp.exp2(s - top)
            es[at[tile], :] = e
            total = total * jnp.exp2(peak - top) + fold(e, jnp.sum)
            peak = top
            peaks.append(peak)
            ps[at[tile], :] = nt(vs[at[tile], :], g)
        inverse = 1.0 / jnp.sum(total, axis=0, keepdims=True)
        shares = [jnp.exp2(old - peak) * inverse for old in peaks]
        delta = jnp.zeros((8, ROWS), F32)
        for tile in range(count):
            w = (es[at[tile], :] * shares[tile]).astype(BF16)
            dv[at[tile], :] += nn(w, g)
            delta += fold(w.astype(F32) * ps[at[tile], :], jnp.sum)
        delta = jnp.sum(delta, axis=0, keepdims=True)
        dq_t = jnp.zeros((HEAD, ROWS), F32)
        for tile in range(count):
            factor = shares[tile] * scaling
            slopes = (es[at[tile], :] * factor * (ps[at[tile], :] - delta)).astype(BF16)
            dk[at[tile], :] += nn(slopes, q)
            dq_t += nn(kt[:, at[tile]], slopes)
        dq = dq_t.T.astype(BF16)
        for index, (turn, h) in enumerate([(turn, h) for turn in turns for h in range(REPEAT)]):
            part = dq[index * HALF : (index + 1) * HALF]
            dqs[turn, :, h * HEAD : (h + 1) * HEAD] = part

    def one_pack(pack, unused):
        turns = [order[0, pack * PACK + i] for i in range(PACK)]
        spans_here = [order[1, pack * PACK + i] for i in range(PACK)]
        tiles = spans_here[-1] * HALF // TILE + 1
        blocks = [rows[turn] for turn in turns]
        cuts = [slice(h * HEAD, (h + 1) * HEAD) for h in range(2 * REPEAT)]
        q = jnp.concatenate([blk[:, cut] for blk in blocks for cut in cuts[:REPEAT]], axis=0)
        g = jnp.concatenate([blk[:, cut] for blk in blocks for cut in cuts[REPEAT:]], axis=0)
        limit = jnp.zeros((1, ROWS), jnp.int32)
        for i in range(PACK):
            limit = jnp.where(lane >= i * REPEAT * HALF, spans_here[i] * HALF, limit)
        limit = limit + lane % HALF
        for count in range(1, SEQ // TILE + 1):
            pl.when(tiles == count)(partial(one_length, count, limit, turns, q, g))
        return unused

    lax.fori_loop(0, 2 * GROUPS // PACK, one_pack, 0)
    for step, ref in enumerate((dq0, dq1, dq2, dq3)):
        for half in range(2):
            ref[half * HALF : (half + 1) * HALF] = dqs[2 * step + half]
    for dc, ref in ((0, keep), (1, send)):
        for chip in range(2 * GROUPS):
            for half in range(2):
                base = pl.multiple_of(spans[4 * chip + 2 * (c ^ dc) + half] * HALF, HALF)
                here = slice(half * HALF, (half + 1) * HALF)
                ref[chip, here, :HEAD] = dk[pl.ds(base, HALF), :].astype(ref.dtype)
                ref[chip, here, HEAD:] = dv[pl.ds(base, HALF), :].astype(ref.dtype)


def attention(spans, token, queries, out_grad, row_pieces, kv_sets):
    return pl.pallas_call(
        attention_kernel,
        out_shape=[struct((TOK, WIDE), BF16)] * GROUPS
        + [
            struct((2 * GROUPS, TOK, 2 * HEAD), BF16),
            struct((2 * GROUPS, TOK, 2 * HEAD), BF16),
        ],
        in_specs=[SMEM, VMEM, ANY, ANY] + [VMEM] * 7,
        out_specs=[VMEM] * 6,
        scratch_shapes=[
            pltpu.VMEM((SEQ, HEAD), BF16),
            pltpu.VMEM((SEQ, HEAD), BF16),
            pltpu.VMEM((HEAD, SEQ), BF16),
            pltpu.VMEM((2 * GROUPS, HALF, 2 * WIDE), BF16),
            pltpu.VMEM((2 * GROUPS, HALF, WIDE), BF16),
            pltpu.VMEM((SEQ, ROWS), F32),
            pltpu.VMEM((SEQ, ROWS), F32),
            pltpu.VMEM((SEQ, HEAD), F32),
            pltpu.VMEM((SEQ, HEAD), F32),
            pltpu.SMEM((2, 2 * GROUPS), jnp.int32),
            pltpu.VMEM((TOK, 2 * WIDE), BF16),
            pltpu.SemaphoreType.DMA((2,)),
        ],
        compiler_params=PARAMS,
        name="attention_backward",
    )(spans, token, queries, out_grad, *row_pieces, *kv_sets)


def join_rows_kernel(p0, p2, p1, p3, out):
    x = lax.axis_index("x")
    for step, ref in ((0, p0), (2, p2), (1, p1), (3, p3)):
        column = pl.multiple_of(((x + step) % GROUPS) * WIDE, WIDE)
        out[:, pl.ds(column, WIDE)] = ref[...]


def join_rows(pieces):
    return pl.pallas_call(
        join_rows_kernel,
        out_shape=struct((TOK, GROUPS * WIDE), BF16),
        in_specs=[VMEM] * GROUPS,
        out_specs=VMEM,
        cost_estimate=LONG,
        compiler_params=PARAMS,
        name="join_rows",
    )(*pieces)


def join_kv(parts):
    split = parts.reshape(GROUPS, 2, TOK, 2 * HEAD).astype(F32)
    total = (split[:, 0] + split[:, 1]).astype(BF16)
    key_grad = total[:, :, :HEAD].transpose(1, 0, 2).reshape(TOK, GROUPS * HEAD)
    value_grad = total[:, :, HEAD:].transpose(1, 0, 2).reshape(TOK, GROUPS * HEAD)
    return key_grad, value_grad


def ahead(block, step):
    return lax.ppermute(block, "x", [(i, (i + step) % GROUPS) for i in range(GROUPS)])


def swap(block, axis):
    return lax.ppermute(block, axis, [(0, 1), (1, 0)])


def on_device(queries, keys, values, out_grad, spans):
    kv0, kv1, kv2, kv3 = cut_kv(keys, values)
    g2 = ahead(kv2, 2)
    kv_mine = jnp.stack([kv0, g2, ahead(kv1, 1), ahead(kv3, 3)])
    rows1, rows2, rows3 = cut_rows(queries, out_grad)
    r2 = ahead(rows2, 2)
    r1, r3 = ahead(rows1, 1), ahead(rows3, 3)
    row_pieces = [r1, r2, r3]
    token = arrived([r2, r1, r3])
    kv_y = swap(kv_mine, "y")
    kv_c = swap(kv_mine, "c")
    kv_yc = swap(kv_y, "c")
    dq0, dq1, dq2, dq3, keep, send = attention(
        spans, token, queries, out_grad, row_pieces, [kv_mine, kv_y, kv_c, kv_yc]
    )
    total = (keep.astype(F32) + swap(send, "c").astype(F32)).astype(BF16)
    home = lax.all_to_all(total, ("x", "y"), 0, 0, tiled=True)
    home2 = ahead(dq2, 2)
    home1, home3 = ahead(dq1, 3), ahead(dq3, 1)
    query_grad = join_rows([dq0, home2, home1, home3])
    key_grad, value_grad = join_kv(home)
    return query_grad, key_grad, value_grad


def solution(mesh):
    split = Mesh(mesh.devices.reshape(-1, 4, 2, 2), ("dp", "x", "y", "c"))
    whole = P(("dp", "x", "y", "c"), None)
    return jax.shard_map(
        on_device,
        mesh=split,
        in_specs=(whole, whole, whole, whole, P("dp")),
        out_specs=(whole, whole, whole),
        check_vma=False,
    )
```
